32 devices in a mesh: groups: 2 (over y), wide: 4 (over z), narrow: 4 (over x, core).
Axes of the slice: x: 2, y: 2, z: 4, core: 2. Of those that a mesh axis runs over, the one named last changes fastest.
Arguments:
- points: float32 [6144, 128], P(('groups', 'wide', 'narrow')), parts along dimension 0, may hold values from -6 to 6
- inv_len: float32 [256], P('groups'), parts along dimension 0, may hold values from 0.02 to 0.2
- amplitude: float32 [2], P('groups'), parts along dimension 0, may hold values from 0.5 to 2
- noise_var: float32 [2], P('groups'), parts along dimension 0, may hold values from 0.5 to 2
- coefficients: float32 [6144, 256], P(('groups', 'wide', 'narrow')), parts along dimension 0, may hold values from -6 to 6
- targets: float32 [6144, 256], P(('groups', 'wide', 'narrow')), parts along dimension 0, may hold values from -50 to 50
- direction_old: float32 [6144, 256], P(('groups', 'wide', 'narrow')), parts along dimension 0, may hold values from -6 to 6
- rr_old: float32 [512], P('groups'), parts along dimension 0, may hold values from 6144 to 49152
Outputs:
- new_coefficients: float32 [6144, 256], P(('groups', 'wide', 'narrow')), parts along dimension 0
- new_residual: float32 [6144, 256], P(('groups', 'wide', 'narrow')), parts along dimension 0
- direction: float32 [6144, 256], P(('groups', 'wide', 'narrow')), parts along dimension 0
- new_norms: float32 [512], P('groups'), parts along dimension 0
The draws below stay inside these ranges and needn't reach their ends.
There are 2 independent parts, one for each index of `groups`. The reference program is written for one: setup_inputs(seed, part) draws one part's arguments, and reference() takes and returns one part's arrays. A program takes and returns all parts, laid end to end along the dimension named above; each array names one. Nothing has to cross between parts.
All inputs are finite; a program needn't handle non-finite values.
Results may differ from the reference program's by a relative error of at most 0.000073.
Values sent between devices are 32-bit elements; how exact they have to be, the bound alone decides.
No kernel may reach another device: no remote copies, remote signals or barrier semaphores. Data moves between devices by JAX's collectives and lax.ppermute only.
A program may use at most 128 MiB of HBM per device.

```python
import math
import jax
import jax.numpy as jnp
from jax import lax

F = 128
S = 256
NPTS = 3072


def draw_targets(key, part):
    first_key, second_key = jax.random.split(jax.random.fold_in(key, 17), 2)
    row_pos = jnp.arange(NPTS, dtype=jnp.float32) / jnp.float32(max(NPTS - 1, 1))
    col_pos = jax.random.uniform(second_key, (S,), jnp.float32)
    row_scale = 10.0 ** (row_pos - 0.5)
    col_scale = 10.0 ** (col_pos - 0.5)
    entries = jnp.clip(jax.random.normal(first_key, (NPTS, S), jnp.float32), -5.0, 5.0)
    return entries * row_scale[:, None] * col_scale[None, :]


def block_scale(key, shape, cuts, low, top_value):
    loudness = 1.0
    for axis_at, blocks in cuts:
        heights = jax.random.uniform(jax.random.fold_in(jax.random.fold_in(key, 6), axis_at), (blocks,), jnp.float32, low / len(cuts), top_value / len(cuts))
        loudness = loudness * jnp.repeat(jnp.exp(heights), shape[axis_at] // blocks).reshape((-1,) + (1,) * (len(shape) - 1 - axis_at))
    return loudness


def normal_values(stream_key, extent, spread, limit, cuts=(), held_as=jnp.bfloat16):
    values = spread * jax.random.normal(stream_key, extent, jnp.float32)
    if cuts:
        values = values * block_scale(stream_key, extent, cuts, -0.22, 0.18)
    return jnp.clip(values, -limit, limit).astype(held_as)


def setup_inputs(seed: int = 0, part: int = 0) -> dict:
    streams_of = jax.random.split(jax.random.key(seed), 9)
    own_keys = jax.random.split(jax.random.fold_in(streams_of[8], part), 9)
    points = normal_values(own_keys[0], (NPTS, F), 1.0, 6.0, ((0, 16),), jnp.float32)
    inv_len = jnp.clip(jnp.exp(jax.random.uniform(own_keys[1], (F,), jnp.float32, math.log(0.02), math.log(0.2))), 0.02, 0.2)
    amplitude = jnp.clip(jax.random.uniform(own_keys[2], (1,), jnp.float32, 0.5, 2.0), 0.5, 2.0)
    noise_var = jnp.clip(jax.random.uniform(own_keys[3], (1,), jnp.float32, 0.5, 2.0), 0.5, 2.0)
    coefficients = normal_values(own_keys[4], (NPTS, S), 1.0, 6.0, ((0, 16),), jnp.float32)
    targets = draw_targets(jax.random.fold_in(jax.random.fold_in(streams_of[8], part), 71), part)
    direction_old = normal_values(own_keys[6], (NPTS, S), 1.0, 6.0, ((0, 16),), jnp.float32)
    rr_old = jnp.clip(jnp.exp(jax.random.uniform(own_keys[7], (S,), jnp.float32, math.log(6144.0), math.log(49152.0))), 6144.0, 49152.0)
    return dict(points=points, inv_len=inv_len, amplitude=amplitude, noise_var=noise_var, coefficients=coefficients, targets=targets, direction_old=direction_old, rr_old=rr_old)


SQRT_FIVE = math.sqrt(5.0)

def matern(squared):
    distance = jnp.sqrt(jnp.maximum(squared, 0.0))
    scaled = SQRT_FIVE * distance
    return (1.0 + scaled + scaled * scaled / 3.0) * jnp.exp(-scaled)

def kernel_apply(scaled_pts, norms_sq, weights, kernel_scale, noise_level):
    block_size = math.gcd(NPTS, 512)
    block_count = NPTS // block_size
    target_blocks = scaled_pts.reshape(block_count, block_size, scaled_pts.shape[1])
    target_norms = norms_sq.reshape(block_count, block_size)

    def one_block(block_pair):
        block_pts, block_norms = block_pair
        cross_dot = lax.dot_general(block_pts, scaled_pts, (((1,), (1,)), ((), ())), precision=lax.Precision.HIGHEST)
        values = matern(block_norms[:, None] + norms_sq[None, :] - 2.0 * cross_dot)
        return jnp.dot(values, weights, precision=lax.Precision.HIGHEST)
    product = lax.map(one_block, (target_blocks, target_norms)).reshape(NPTS, weights.shape[1])
    return kernel_scale * product + noise_level * weights

def reference(points, inv_len, amplitude, noise_var, coefficients, targets, direction_old, rr_old):
    scaled_pts = points * inv_len[None, :]
    norms_sq = lax.optimization_barrier(jnp.sum(scaled_pts * scaled_pts, axis=1))
    kernel_scale = amplitude[0] / math.sqrt(NPTS)
    noise_level = noise_var[0]
    residual = targets - kernel_apply(scaled_pts, norms_sq, coefficients, kernel_scale, noise_level)
    rr_now = lax.optimization_barrier(jnp.sum(residual * residual, axis=0))
    direction = residual + (rr_now / rr_old)[None, :] * direction_old
    image_dir = kernel_apply(scaled_pts, norms_sq, direction, kernel_scale, noise_level)
    step_size = rr_now / lax.optimization_barrier(jnp.sum(direction * image_dir, axis=0))
    new_coefficients = coefficients + step_size[None, :] * direction
    new_residual = residual - step_size[None, :] * image_dir
    new_norms = lax.optimization_barrier(jnp.sum(new_residual * new_residual, axis=0))
    return (new_coefficients, new_residual, direction, new_norms)
```

```python
import math

import jax
import jax.numpy as jnp
from jax import lax
from jax.sharding import PartitionSpec as P

SQRT_FIVE = math.sqrt(5.0)
AXES = ("wide", "narrow")
PREC = lax.Precision.HIGHEST


def matern(squared):
    distance = jnp.sqrt(jnp.maximum(squared, 0.0))
    scaled = SQRT_FIVE * distance
    return (1.0 + scaled + scaled * scaled / 3.0) * jnp.exp(-scaled)


def swap(value, mask, ndev):
    return lax.ppermute(value, AXES, [(i, i ^ mask) for i in range(ndev)])


def masks_of(bits):
    out = [0]
    for bit in bits:
        out += [m | (1 << bit) for m in out]
    return sorted(out)


def local(points, inv_len, amplitude, noise_var, coefficients, targets, direction_old, rr_old):
    rows = points.shape[0]
    ndev = lax.axis_size("wide") * lax.axis_size("narrow")
    nbits = ndev.bit_length() - 1
    bits_a = list(range(1, 1 + nbits // 2))
    bits_b = [0] + list(range(1 + nbits // 2, nbits))
    high_b = bits_b[1:]
    masks_a = masks_of(bits_a)
    masks_b = masks_of(bits_b)
    masks_h = masks_of(high_b)
    kernel_scale = amplitude[0] * (1.0 / math.sqrt(rows * ndev))
    noise_level = noise_var[0]

    def gather_b(value):
        parts = {0: value}
        for bit in high_b:
            parts.update({m | 1 << bit: swap(v, 1 << bit, ndev) for m, v in list(parts.items())})
        high = jnp.concatenate([parts[m] for m in masks_h], axis=0)
        other = swap(high, 1, ndev)
        chunks = {}
        for i, m in enumerate(masks_h):
            chunks[m] = parts[m]
            chunks[m | 1] = other[i * rows:(i + 1) * rows]
        return jnp.concatenate([chunks[m] for m in masks_b], axis=0)

    own_pts = points * inv_len[None, :]
    pts_a = jnp.concatenate([own_pts] + [swap(own_pts, m, ndev) for m in masks_a[1:]], axis=0)
    pts_b = gather_b(own_pts)
    coef_a = jnp.concatenate([coefficients] + [swap(coefficients, m, ndev) for m in masks_a[1:]], axis=0)
    dir_b = gather_b(direction_old)
    cross = lax.dot_general(pts_b, pts_a, (((1,), (1,)), ((), ())), precision=PREC)
    norms_a = jnp.sum(pts_a * pts_a, axis=1)
    norms_b = jnp.sum(pts_b * pts_b, axis=1)
    values = matern(norms_b[:, None] + norms_a[None, :] - 2.0 * cross)

    def block(stack, i):
        return stack[i * rows:(i + 1) * rows]

    def apply_t(weights):
        return lax.dot_general(values, weights, (((0,), (0,)), ((), ())), precision=PREC)

    def settle_a(part):
        total = block(part, 0)
        for i, m in enumerate(masks_a):
            if m:
                total = total + swap(block(part, i), m, ndev)
        return total

    image_old = kernel_scale * settle_a(apply_t(dir_b)) + noise_level * direction_old
    partial = -kernel_scale * jnp.dot(values, coef_a, precision=PREC)
    keep = jnp.concatenate([block(partial, i) for i, m in enumerate(masks_b) if not m & 1], axis=0)
    give = jnp.concatenate([block(partial, i) for i, m in enumerate(masks_b) if m & 1], axis=0)
    keep = keep + swap(give, 1, ndev)
    keep = keep.at[:rows].add(targets - noise_level * coefficients)
    for bit in high_b:
        other = swap(keep, 1 << bit, ndev)
        pos = {m: i for i, m in enumerate(masks_h)}
        keep = keep + jnp.concatenate([block(other, pos[m ^ 1 << bit]) for m in masks_h], axis=0)
    other = swap(keep, 1, ndev)
    residual = keep[:rows]
    chunks = {}
    for i, m in enumerate(masks_h):
        chunks[m], chunks[m | 1] = block(keep, i), block(other, i)
    res_b = jnp.concatenate([chunks[m] for m in masks_b], axis=0)
    image_new = kernel_scale * settle_a(apply_t(res_b)) + noise_level * residual

    def dot(a, b):
        return jnp.sum(a * b, axis=0)

    sums = jnp.stack([
        dot(residual, residual),
        dot(residual, image_new),
        dot(residual, image_old),
        dot(direction_old, image_new),
        dot(direction_old, image_old),
        dot(image_new, image_new),
        dot(image_new, image_old),
        dot(image_old, image_old),
    ])
    for bit in range(nbits):
        sums = sums + swap(sums, 1 << bit, ndev)
    rr_now, ra, rb, da, db, aa, ab, bb = (sums[i] for i in range(8))
    ratio = rr_now / rr_old
    curvature = ra + ratio * (rb + da) + ratio * ratio * db
    cross_sum = ra + ratio * rb
    image_sum = aa + 2.0 * ratio * ab + ratio * ratio * bb
    step_size = rr_now / curvature
    direction = residual + ratio[None, :] * direction_old
    image_dir = image_new + ratio[None, :] * image_old
    new_residual = residual - step_size[None, :] * image_dir
    new_norms = rr_now - 2.0 * step_size * cross_sum + step_size * step_size * image_sum
    new_coefficients = coefficients + step_size[None, :] * direction
    return (new_coefficients, new_residual, direction, new_norms)


def solution(mesh):
    rows = P(("groups", "wide", "narrow"), None)
    return jax.shard_map(
        local,
        mesh=mesh,
        in_specs=(rows, P("groups"), P("groups"), P("groups"), rows, rows, rows, P("groups")),
        out_specs=(rows, rows, rows, P("groups")),
        check_vma=False,
    )
```
